256 devices in a mesh: head: 8 (over x_hi, y), tok: 32 (over z, x_lo, core).
Axes of the slice: x: 4 (x_hi: 2, x_lo: 2; x = x_hi * 2 + x_lo), y: 4, z: 8, core: 2. Of those that a mesh axis runs over, the one named last changes fastest.
Arguments:
- tokens: bfloat16 [16384, 8192], P('tok', 'head'), may hold values from -20 to 20
- qkv_maps: bfloat16 [16, 512, 1536], P('head'), may hold values from -0.26516504 to 0.26516504
- rate_map: bfloat16 [8192, 16], P('head'), may hold values from -0.09375 to 0.09375
- fast_init: bfloat16 [16, 3, 512, 512], P('head'), may hold values from -0.25 to 0.25
Outputs:
- layer_out: bfloat16 [16384, 8192], P('tok', 'head')
The draws below stay inside these ranges and needn't reach their ends.
All inputs are finite; a program needn't handle non-finite values.
Results may differ from the reference program's by a relative error of at most 0.04.
Values may be sent and summed in bfloat16 or wider, within the bound.
A program may use at most 128 MiB of HBM per device.

```python
import jax
import jax.numpy as jnp
from jax import lax

H = 16
HD = 512
WINDOW = 512
TOK_DEV = 512
D = 8192
TOKENS = 16384
STRETCH = 8192
PIECE = 16
N_TOK = 32


def draw_tokens(key, part):
    keys = jax.random.split(jax.random.fold_in(key, 17), 1)
    return jnp.clip(jax.random.normal(keys[0], (TOKENS, D), jnp.float32), -6.0, 6.0).astype(jnp.bfloat16)


def draw_qkv_maps(key, part):
    keys = jax.random.split(jax.random.fold_in(key, 29), 3)
    shape = (H, HD, HD)
    factor = HD ** (-0.5)
    query_map = jnp.clip(jax.random.normal(keys[0], shape, jnp.float32), -5.0, 5.0) * factor
    own_key = jnp.clip(jax.random.normal(keys[1], shape, jnp.float32), -5.0, 5.0) * factor
    value_map = jnp.clip(jax.random.normal(keys[2], shape, jnp.float32), -5.0, 5.0) * factor
    key_map = own_key
    return jnp.concatenate([query_map, key_map, value_map], 2).astype(jnp.bfloat16)


def spiked(drawn, key, source, target, blocks, factor):
    def block_of(dim):
        return (jnp.arange(drawn.shape[dim]) // (drawn.shape[dim] // blocks)).reshape((-1,) + (1,) * (drawn.ndim - 1 - dim))

    near = jax.random.permutation(key, blocks)[block_of(target)]
    second = (block_of(target) + blocks // 2) % blocks
    return jnp.where((block_of(source) == near) | (block_of(source) == second), factor * drawn, drawn)


def levels(key, extent, cuts, smallest, largest):
    def one(axis_at, shards_of):
        heights = jax.random.uniform(jax.random.fold_in(jax.random.fold_in(key, 6), axis_at), (shards_of,), jnp.float32, smallest / len(cuts), largest / len(cuts))
        return jnp.repeat(jnp.exp(heights), extent[axis_at] // shards_of).reshape((-1,) + (1,) * (len(extent) - axis_at - 1))

    factor_of = one(*cuts[0])
    for cut in cuts[1:]:
        factor_of = factor_of * one(*cut)
    return factor_of


def scatter_about(key, extent, deviation, limit, shards=(), kind=jnp.bfloat16):
    entries = jax.random.normal(key, extent, jnp.float32) * deviation
    if len(shards) > 0:
        entries = levels(key, extent, shards, -0.22, 0.18) * entries
    return jnp.clip(entries, min=-limit, max=limit).astype(kind)


def gaussian_with(rng, extent, width, bound, shards, heavy, held_as=jnp.bfloat16):
    values = width * jax.random.normal(rng, extent, jnp.float32)
    if shards:
        values = values * levels(rng, extent, shards, -0.22, 0.18)
    return jnp.clip(spiked(values, jax.random.fold_in(rng, 3), *heavy), -bound, bound).astype(held_as)


def setup_inputs(seed: int = 0) -> dict:
    splits = jax.random.split(jax.random.key(seed), 5)
    tokens = draw_tokens(jax.random.fold_in(splits[4], 71), 0)
    qkv_maps = draw_qkv_maps(jax.random.fold_in(splits[4], 71), 0)
    rate_map = gaussian_with(splits[2], (D, H), D ** -0.5, 0.09375, ((0, 8),), (0, 1, 8, 2.0))
    fast_init = scatter_about(splits[3], (H, 3, HD, HD), HD ** -0.5, 0.25, ((0, 8),))
    return dict(tokens=tokens, qkv_maps=qkv_maps, rate_map=rate_map, fast_init=fast_init)


rate_base = 0.003
epsilon = 1e-06

def rms_rows(matrix):
    matrix = matrix.astype(jnp.float32)
    return matrix / jnp.sqrt(lax.optimization_barrier(jnp.mean(matrix * matrix, axis=-1, keepdims=True)) + epsilon)

def renorm(updated, initial):
    target = jnp.sqrt(lax.optimization_barrier(jnp.mean(initial * initial, axis=-1, keepdims=True)) + epsilon)
    current = jnp.sqrt(lax.optimization_barrier(jnp.mean(updated * updated, axis=-1, keepdims=True)) + epsilon)
    return (updated * (target / current)).astype(jnp.bfloat16)

def settle(array):
    return lax.optimization_barrier(array.astype(jnp.bfloat16)).astype(jnp.float32)

def band_attention(queries, key_rows, value_rows):
    zeros = jnp.zeros((WINDOW, HD), jnp.bfloat16)
    padded_keys = jnp.concatenate([zeros, key_rows], 0)
    padded_values = jnp.concatenate([zeros, value_rows], 0)
    score_scale = HD ** (-0.5)

    def one_span(span_index):
        start = span_index * TOK_DEV
        query_span = lax.dynamic_slice_in_dim(queries, start, TOK_DEV, 0)
        key_span = lax.dynamic_slice_in_dim(padded_keys, start, TOK_DEV + WINDOW, 0)
        value_span = lax.dynamic_slice_in_dim(padded_values, start, TOK_DEV + WINDOW, 0)
        scores = jnp.dot(query_span, key_span.T, preferred_element_type=jnp.float32) * score_scale
        query_pos = start + jnp.arange(TOK_DEV, dtype=jnp.int32)
        key_pos = start - WINDOW + jnp.arange(TOK_DEV + WINDOW, dtype=jnp.int32)
        key_mask = (key_pos[None, :] <= query_pos[:, None]) & (key_pos[None, :] > query_pos[:, None] - WINDOW) & (key_pos[None, :] >= 0)
        row_max = lax.optimization_barrier(jnp.max(jnp.where(key_mask, scores, -1e+30), axis=1, keepdims=True))
        raised = jnp.where(key_mask, jnp.exp(scores - row_max), 0.0)
        probs = (raised / lax.optimization_barrier(jnp.sum(raised, axis=1, keepdims=True))).astype(jnp.bfloat16)
        return jnp.dot(probs, value_span, preferred_element_type=jnp.float32)
    spans = lax.map(one_span, jnp.arange(TOKENS // TOK_DEV, dtype=jnp.int32))
    return spans.reshape(TOKENS, HD)

def regroup(array):
    shaped = array.reshape((N_TOK // 2, N_TOK, PIECE) + array.shape[1:])
    shaped = jnp.swapaxes(shaped, 0, 1)
    return shaped.reshape((N_TOK, N_TOK // 2 * PIECE) + array.shape[1:])

def fast_head(q_norm, k_norm, value_rows, rate_row, fast_weights):
    initial = fast_weights.astype(jnp.float32)
    weights = fast_weights
    outputs = []
    for half_index in range(2):
        first = half_index * STRETCH
        key_groups = regroup(k_norm[first:first + STRETCH]).astype(jnp.float32)
        value_groups = regroup(value_rows[first:first + STRETCH]).astype(jnp.float32)
        rate_groups = regroup(rate_row[first:first + STRETCH]).astype(jnp.float32)
        current = weights.astype(jnp.float32)
        pre_gate = jnp.einsum('jrd,de->jre', key_groups, current[0])
        pre_up = jnp.einsum('jrd,de->jre', key_groups, current[1])
        sigma = jax.nn.sigmoid(pre_gate)
        gated = pre_gate * sigma
        hidden = settle(gated * pre_up)
        target = settle(rate_groups[:, :, None] * value_groups)
        grad_down = jnp.einsum('jre,jrd->jed', hidden, target)
        back_hidden = jnp.einsum('jrd,ed->jre', target, current[2])
        gate_delta = settle(back_hidden * pre_up * sigma * (1.0 + pre_gate * (1.0 - sigma)))
        up_delta = settle(back_hidden * gated)
        grad_gate = jnp.einsum('jrd,jre->jde', key_groups, gate_delta)
        grad_up = jnp.einsum('jrd,jre->jde', key_groups, up_delta)
        partials = settle(jnp.stack([grad_gate, grad_up, grad_down], 1))
        weights = renorm(current + lax.optimization_barrier(jnp.sum(partials, 0)), initial)
        query_rows = q_norm[first:first + STRETCH]
        app_gate = jnp.dot(query_rows, weights[0], preferred_element_type=jnp.float32)
        app_up = jnp.dot(query_rows, weights[1], preferred_element_type=jnp.float32)
        app_hidden = (app_gate * jax.nn.sigmoid(app_gate) * app_up).astype(jnp.bfloat16)
        outputs.append(jnp.dot(app_hidden, weights[2], preferred_element_type=jnp.float32).astype(jnp.bfloat16))
    return jnp.concatenate(outputs, 0)

def reference(tokens, qkv_maps, rate_map, fast_init):
    logits = jnp.dot(tokens, rate_map, preferred_element_type=jnp.float32)
    rate = (rate_base * jax.nn.softplus(logits)).astype(jnp.bfloat16)
    head_inputs = jnp.swapaxes(tokens.reshape(TOKENS, H, HD), 0, 1)

    def per_head(items):
        inputs, maps, rate_row, fast_weights = items
        projected = jnp.dot(inputs, maps, preferred_element_type=jnp.float32)
        queries = projected[:, :HD].astype(jnp.bfloat16)
        key_rows = projected[:, HD:2 * HD].astype(jnp.bfloat16)
        value_rows = projected[:, 2 * HD:].astype(jnp.bfloat16)
        attended = band_attention(queries, key_rows, value_rows)
        q_norm = rms_rows(queries).astype(jnp.bfloat16)
        k_norm = rms_rows(key_rows).astype(jnp.bfloat16)
        fast = fast_head(q_norm, k_norm, value_rows, rate_row, fast_weights)
        return (attended + fast.astype(jnp.float32)).astype(jnp.bfloat16)
    result = lax.map(per_head, (head_inputs, qkv_maps, rate.T, fast_init))
    return jnp.swapaxes(result, 0, 1).reshape(TOKENS, D)
```

```python
import functools

import jax
import jax.numpy as jnp
from jax import lax
from jax.experimental import pallas as pl
from jax.experimental.pallas import tpu as pltpu
from jax.sharding import PartitionSpec as P

MESH = pl.DeviceIdType.MESH
WINDOW = 512
HD = 512
HALF = 256
ROWS = 512
NC = 8
NZ = 8
NH = 8
CH = 96

rate_base = 0.003
epsilon = 1e-06

bf16 = jnp.bfloat16
f32 = jnp.float32


def dot(a, b):
    return jnp.dot(a, b, preferred_element_type=f32)


def dot_t(a, b):
    return lax.dot_general(a, b, (((1,), (1,)), ((), ())), preferred_element_type=f32)


def dot_l(a, b):
    return lax.dot_general(a, b, (((0,), (0,)), ((), ())), preferred_element_type=f32)


def softplus(a):
    return jnp.maximum(a, 0.0) + jnp.log1p(jnp.exp(-jnp.abs(a)))


def rms(m):
    m = m.astype(f32)
    return (m * lax.rsqrt(jnp.mean(m * m, axis=-1, keepdims=True) + epsilon)).astype(bf16)


def learn_kernel(
    tok_ref, maps_ref, rmap_ref, init_ref,
    wall, halo,
    xbuf, knb, vb, dbuf, g13, g2, rbuf, sbuf, wp, wcur, ss_s, ss_r,
    rcol, lgs, lgr, rates,
    xp_s, xp_r, xx_s, xx_r, xf_s, xf_r, lg_s, lg_r, rt_s, rt_r,
    rs_s, rs_r, sp_s, sp_r, wn_s, wn_r, wc_s, wc_r,
    dp_s, dp_r, dx_s, dx_r, df_s, df_r, ha_s, ha_r,
):
    head = lax.axis_index("head")
    tok = lax.axis_index("tok")
    z = tok // 4
    x = (tok // 2) % 2
    c = tok % 2
    p = z % 4
    s = z // 4
    b_me = x * 2 + c

    def at(zz, xx, cc):
        return (head, zz * 4 + xx * 2 + cc)

    up = at((z + 1) % NZ, x, c)
    down = at((z + NZ - 1) % NZ, x, c)
    mate = at(z, x, 1 - c)
    side = at(z, 1 - x, c)
    diag = at(z, 1 - x, 1 - c)
    tok_next = (head, (tok + 1) % 32)
    tok_prev = (head, (tok + 31) % 32)

    barrier = pltpu.get_barrier_semaphore()
    peers = [up, down, mate, side, diag, tok_next, tok_prev]
    peers += [((head + o) % NH, tok) for o in range(1, NH)]
    for peer in peers:
        pl.semaphore_signal(barrier, inc=1, device_id=peer, device_id_type=MESH)
    pl.semaphore_wait(barrier, len(peers))

    def rcopy(src, dst, ssem, rsem, dev):
        return pltpu.make_async_remote_copy(
            src_ref=src, dst_ref=dst, send_sem=ssem, recv_sem=rsem,
            device_id=dev, device_id_type=MESH,
        )

    mine = pl.ds(pl.multiple_of(x * HD, HD), HD)
    other = pl.ds(pl.multiple_of((1 - x) * HD, HD), HD)

    def x_send(j):
        return rcopy(
            tok_ref.at[pl.ds(j * 128, 128), other],
            xbuf.at[b_me, pl.ds(j * 128, 128)],
            xx_s.at[j], xx_r.at[j], side,
        )

    def x_recv(j):
        return rcopy(
            tok_ref.at[pl.ds(j * 128, 128), other],
            xbuf.at[(1 - x) * 2 + c, pl.ds(j * 128, 128)],
            xx_s.at[j], xx_r.at[j], side,
        )

    def f_send(j):
        blk = xbuf.at[(1 - x) * 2 + c, pl.ds(j * 128, 128)]
        return rcopy(blk, blk, xf_s.at[j], xf_r.at[j], mate)

    def f_recv(j):
        blk = xbuf.at[(1 - x) * 2 + 1 - c, pl.ds(j * 128, 128)]
        return rcopy(blk, blk, xf_s.at[j], xf_r.at[j], mate)

    p_send = rcopy(tok_ref.at[:, mine], xbuf.at[b_me], xp_s, xp_r, mate)
    p_recv = rcopy(tok_ref.at[:, mine], xbuf.at[x * 2 + 1 - c], xp_s, xp_r, mate)
    for j in range(4):
        x_send(j).start()
    p_send.start()
    xbuf[b_me] = tok_ref[:, mine]

    part = lax.dot_general(
        rmap_ref[...], tok_ref[...], (((0,), (1,)), ((), ())), preferred_element_type=f32
    )
    for q in range(NH):
        lgs[q] = jnp.concatenate([part[2 * q : 2 * q + 2], jnp.zeros((6, ROWS), f32)], 0)

    def lg_copy(o):
        peer = (head + o) % NH
        return rcopy(lgs.at[peer], lgr.at[head], lg_s.at[o - 1], lg_r.at[head], (peer, tok))

    def lg_wait(o):
        src = (head + o) % NH
        return rcopy(lgs.at[src], lgr.at[src], lg_s.at[o - 1], lg_r.at[src], (src, tok))

    for o in range(1, NH):
        lg_copy(o).start()
    lgr[head] = lgs[head]

    def keys_values(b):
        def step(i, carry):
            rows = pl.ds(pl.multiple_of(i * 256, 256), 256)
            xb = xbuf[b, rows]
            out = pl.ds(pl.multiple_of(b * ROWS + i * 256, 256), 256)
            knb[out] = rms(dot(xb, maps_ref[x, :, HD : 2 * HD]).astype(bf16))
            vb[out] = dot(xb, maps_ref[x, :, 2 * HD :]).astype(bf16)
            return carry

        lax.fori_loop(0, 2, step, 0)

    keys_values(b_me)

    for o in range(1, NH):
        lg_wait(o).wait_recv()
    total = lgr[0]
    for q in range(1, NH):
        total = total + lgr[q]
    rates[b_me] = (rate_base * softplus(total)).astype(bf16).astype(f32)
    group = [(mate, x * 2 + 1 - c), (side, (1 - x) * 2 + c), (diag, (1 - x) * 2 + 1 - c)]

    def rt_copy(i):
        dev, _ = group[i]
        return rcopy(rates.at[b_me], rates.at[b_me], rt_s.at[i], rt_r.at[b_me], dev)

    def rt_wait(i):
        dev, src = group[i]
        return rcopy(rates.at[src], rates.at[src], rt_s.at[i], rt_r.at[src], dev)

    for i in range(3):
        rt_copy(i).start()

    p_recv.wait_recv()
    keys_values(x * 2 + 1 - c)
    for j in range(4):
        x_recv(j).wait_recv()
        f_send(j).start()
    keys_values((1 - x) * 2 + c)
    for j in range(4):
        f_recv(j).wait_recv()
    keys_values((1 - x) * 2 + 1 - c)

    for i in range(3):
        rt_wait(i).wait_recv()
    for b in range(4):
        row = jnp.where(x == 0, rates[b, 0:1], rates[b, 1:2])
        rcol[b * ROWS : (b + 1) * ROWS] = jnp.broadcast_to(row, (128, ROWS)).T

    ha_copy = rcopy(tok_ref, halo, ha_s, ha_r, tok_next)

    @pl.when((s == 1) & (tok < 31))
    def _():
        ha_copy.start()

    cols = pl.ds(pl.multiple_of(c * HALF, HALF), HALF)

    @pl.when(s == 0)
    def _():
        def fill(j, carry):
            for d in range(2):
                r32 = pl.ds(pl.multiple_of(d * 256 + j * 32, 32), 32)
                r16 = pl.ds(pl.multiple_of(c * HALF + d * 128 + j * 16, 16), 16)
                wcur[d, j, 0:32] = init_ref[x, 0, r32, cols]
                wcur[d, j, 32:64] = init_ref[x, 1, r32, cols]
                wcur[d, j, 64:80] = init_ref[x, 2, r16, 0:HALF]
                wcur[d, j, 80:96] = init_ref[x, 2, r16, HALF:]
            return carry

        lax.fori_loop(0, NC, fill, 0)

    def wc_copy(d, j, src):
        dev = up if d == 0 else down
        return rcopy(src, wcur.at[d, j], wc_s.at[d, j], wc_r.at[d, j], dev)

    @pl.when(s == 1)
    def _():
        def step(i, carry):
            for d in range(2):
                hop = z - 4 if d == 0 else 7 - z
                j = i - hop

                @pl.when((j >= 0) & (j < NC))
                def _():
                    wc_copy(d, j, wcur.at[d, j]).wait_recv()

                    @pl.when(hop < 3)
                    def _():
                        wc_copy(d, j, wcur.at[d, j]).start()

            return carry

        lax.fori_loop(0, NC + 3, step, 0)

    def inner(i, carry):
        rows = pl.ds(pl.multiple_of(i * 256, 256), 256)
        kn = knb[rows]
        v = vb[rows]
        w1 = wcur[:, :, 0:32].reshape(HD, HALF)
        w3 = wcur[:, :, 32:64].reshape(HD, HALF)
        w2a = wcur[:, :, 64:80].reshape(HALF, HALF)
        w2b = wcur[:, :, 80:96].reshape(HALF, HALF)
        h1 = dot(kn, w1)
        h3 = dot(kn, w3)
        back = dot_t(v[:, :HALF], w2a) + dot_t(v[:, HALF:], w2b)
        r = rcol[rows]
        r = jnp.concatenate([r, r], 1)
        sig = jax.nn.sigmoid(h1)
        gated = h1 * sig
        back = back * r
        dbuf[rows, 0:HALF] = (back * h3 * sig * (1.0 + h1 * (1.0 - sig))).astype(bf16)
        dbuf[rows, HALF : 2 * HALF] = (back * gated).astype(bf16)
        dbuf[rows, 2 * HALF :] = (gated * h3 * r).astype(bf16)
        return carry

    lax.fori_loop(0, 8, inner, 0)

    def outer(i, carry):
        rows = pl.ds(pl.multiple_of(i * 256, 256), 256)
        g13[rows] = dot_l(knb[:, rows], dbuf[:, : 2 * HALF])
        return carry

    lax.fori_loop(0, 2, outer, 0)
    g2[...] = dot_l(dbuf[:, 2 * HALF :], vb[...])

    def own_part(d, j):
        r32 = pl.ds(pl.multiple_of(d * 256 + j * 32, 32), 32)
        r16 = pl.ds(pl.multiple_of(d * 128 + j * 16, 16), 16)
        return jnp.concatenate(
            [g13[r32, :HALF], g13[r32, HALF:], g2[r16, :HALF], g2[r16, HALF:]], 0
        )

    def rs_copy(d, j):
        dev = up if d == 0 else down
        return rcopy(sbuf.at[d, j], rbuf.at[d, j], rs_s.at[d, j], rs_r.at[d, j], dev)

    def sp_copy(d, j):
        return rcopy(ss_s.at[d, j], ss_r.at[d, j], sp_s.at[d, j], sp_r.at[d, j], mate)

    def wn_copy(d, j):
        dev = down if d == 0 else up
        w = wall.at[x, c, d, j]
        return rcopy(w, w, wn_s.at[d, j], wn_r.at[d, j], dev)

    def dp_copy(d, j):
        w = wall.at[x, c, d, j]
        return rcopy(w, w, dp_s.at[d, j], dp_r.at[d, j], mate)

    def dx_copy(d, j):
        w = wall.at[x, c, d, j]
        return rcopy(w, w, dx_s.at[d, j], dx_r.at[d, j], side)

    def df_copy(d, j):
        w = wall.at[1 - x, c, d, j]
        return rcopy(w, w, df_s.at[d, j], df_r.at[d, j], mate)

    def spread(d, j):
        dp_copy(d, j).start()
        dx_copy(d, j).start()

    def pos(d):
        return p if d == 0 else 3 - p

    def rs_stage(d, j):
        @pl.when((j >= 0) & (j < NC))
        def _():
            q = pos(d)

            @pl.when(q == 0)
            def _():
                sbuf[d, j] = own_part(d, j).astype(bf16)
                rs_copy(d, j).start()

            @pl.when((q > 0) & (q < 3))
            def _():
                rs_copy(d, j).wait_recv()
                sbuf[d, j] = (own_part(d, j) + rbuf[d, j].astype(f32)).astype(bf16)
                rs_copy(d, j).start()

            @pl.when(q == 3)
            def _():
                rs_copy(d, j).wait_recv()
                w = own_part(d, j) + rbuf[d, j].astype(f32) + wcur[d, j].astype(f32)
                wp[d, j] = w
                sq = w[0:64] * w[0:64]
                ss_s[d, j] = sq[:, :128] + sq[:, 128:]
                sp_copy(d, j).start()

    def fin_stage(d, j):
        @pl.when((j >= 0) & (j < NC) & (pos(d) == 3))
        def _():
            sp_copy(d, j).wait_recv()
            w = wp[d, j]
            r32 = pl.ds(pl.multiple_of(d * 256 + j * 32, 32), 32)
            r16 = pl.ds(pl.multiple_of(c * HALF + d * 128 + j * 16, 16), 16)
            i1 = init_ref[x, 0, r32].astype(f32)
            i3 = init_ref[x, 1, r32].astype(f32)
            i2 = init_ref[x, 2, r16].astype(f32)
            i13 = jnp.concatenate([i1, i3], 0)
            want = jnp.sqrt(jnp.mean(i13 * i13, axis=1, keepdims=True) + epsilon)
            have = jnp.sum(ss_s[d, j] + ss_r[d, j], axis=1, keepdims=True) * (1.0 / HD)
            wall[x, c, d, j, 0:64] = (w[0:64] * (want / jnp.sqrt(have + epsilon))).astype(bf16)
            want2 = jnp.sqrt(jnp.mean(i2 * i2, axis=1, keepdims=True) + epsilon)
            wa, wb = w[64:80], w[80:96]
            have2 = jnp.sum(wa * wa + wb * wb, axis=1, keepdims=True) * (1.0 / HD)
            scale2 = want2 / jnp.sqrt(have2 + epsilon)
            wall[x, c, d, j, 64:80] = (wa * scale2).astype(bf16)
            wall[x, c, d, j, 80:96] = (wb * scale2).astype(bf16)

            @pl.when(s == 0)
            def _():
                wc_copy(d, j, wall.at[x, c, d, j]).start()

            wn_copy(d, j).start()
            spread(d, j)

    def ag_stage(d, j):
        @pl.when((j >= 0) & (j < NC) & (pos(d) < 3))
        def _():
            wn_copy(d, j).wait_recv()

            @pl.when(pos(d) > 0)
            def _():
                wn_copy(d, j).start()

            spread(d, j)

    def pipe(i, carry):
        for d in range(2):
            rs_stage(d, i - pos(d))
        for d in range(2):
            fin_stage(d, i - 4)
        for d in range(2):
            ag_stage(d, i - 5 - (3 - pos(d)))
        return carry

    lax.fori_loop(0, NC + 8, pipe, 0)

    @pl.when((s == 0))
    def _():
        ha_copy.start()

    @pl.when(tok == 0)
    def _():
        halo[...] = jnp.zeros_like(halo)

    def gather(j, carry):
        for d in range(2):
            w = wall.at[1 - x, c, d, j]
            rcopy(w, w, dx_s.at[d, j], dx_r.at[d, j], side).wait_recv()
            df_copy(d, j).start()
        return carry

    lax.fori_loop(0, NC, gather, 0)

    def finish(j, carry):
        for d in range(2):
            w = wall.at[x, 1 - c, d, j]
            rcopy(w, w, dp_s.at[d, j], dp_r.at[d, j], mate).wait_recv()
            w = wall.at[1 - x, 1 - c, d, j]
            rcopy(w, w, df_s.at[d, j], df_r.at[d, j], mate).wait_recv()
            dp_copy(d, j).wait_send()
            dx_copy(d, j).wait_send()
            df_copy(d, j).wait_send()
            q = pos(d)

            @pl.when(q < 3)
            def _():
                rs_copy(d, j).wait_send()

            @pl.when(q == 3)
            def _():
                sp_copy(d, j).wait_send()

            @pl.when(q > 0)
            def _():
                wn_copy(d, j).wait_send()

            hop = z - 4 if d == 0 else 7 - z

            @pl.when(((s == 0) & (q == 3)) | ((s == 1) & (hop < 3)))
            def _():
                wc_copy(d, j, wcur.at[d, j]).wait_send()

        return carry

    lax.fori_loop(0, NC, finish, 0)
    p_send.wait_send()
    for j in range(4):
        x_send(j).wait_send()
        f_send(j).wait_send()
    for o in range(1, NH):
        lg_copy(o).wait_send()
    for i in range(3):
        rt_copy(i).wait_send()

    @pl.when(tok < 31)
    def _():
        ha_copy.wait_send()

    @pl.when(tok > 0)
    def _():
        ha_copy.wait_recv()


def apply_kernel(tok_ref, halo_ref, maps_ref, wall, out_ref, kb, vb):
    first = lax.axis_index("tok") == 0

    def one(it, carry):
        h = it
        lanes = pl.ds(pl.multiple_of(h * HD, HD), HD)

        def kv(i, cc):
            src = pl.ds(pl.multiple_of(i * 256, 256), 256)
            for ref, base in ((halo_ref, 0), (tok_ref, ROWS)):
                dst = pl.ds(pl.multiple_of(base + i * 256, 256), 256)
                xb = ref[src, lanes]
                kb[dst] = dot(xb, maps_ref[h, :, HD : 2 * HD]).astype(bf16)
                vb[dst] = dot(xb, maps_ref[h, :, 2 * HD :]).astype(bf16)
            return cc

        lax.fori_loop(0, 2, kv, 0)

        def block(i, cc):
            rows = pl.ds(pl.multiple_of(i * 256, 256), 256)
            keys = pl.ds(pl.multiple_of(i * 256, 256), 768)
            q = dot(tok_ref[rows, lanes], maps_ref[h, :, 0:HD]).astype(bf16)
            sc = dot_t(q, kb[keys]) * (HD ** (-0.5))
            ri = lax.broadcasted_iota(jnp.int32, (256, 768), 0)
            ki = lax.broadcasted_iota(jnp.int32, (256, 768), 1)
            low = jnp.where(first, WINDOW - i * 256, 0)
            mask = (ki > ri) & (ki <= ri + WINDOW) & (ki >= low)
            top = jnp.max(jnp.where(mask, sc, -1e30), axis=1, keepdims=True)
            e = jnp.where(mask, jnp.exp(sc - top), 0.0)
            probs = (e / jnp.sum(e, axis=1, keepdims=True)).astype(bf16)
            att = dot(probs, vb[keys])
            qn = rms(q)
            fast = None
            for c in range(2):
                w1 = wall[h, c, :, :, 0:32].reshape(HD, HALF)
                w3 = wall[h, c, :, :, 32:64].reshape(HD, HALF)
                w2a = wall[h, c, :, :, 64:80].reshape(HALF, HALF)
                w2b = wall[h, c, :, :, 80:96].reshape(HALF, HALF)
                a1 = dot(qn, w1)
                hq = (a1 * jax.nn.sigmoid(a1) * dot(qn, w3)).astype(bf16)
                f = jnp.concatenate([dot(hq, w2a), dot(hq, w2b)], 1)
                fast = f if fast is None else fast + f
            out_ref[rows, lanes] = (att + fast.astype(bf16).astype(f32)).astype(bf16)
            return cc

        lax.fori_loop(0, 2, block, 0)
        return carry

    lax.fori_loop(0, 2, one, 0)


def body(tokens, qkv_maps, rate_map, fast_init):
    vm = pl.BlockSpec(memory_space=pltpu.VMEM)
    dma = pltpu.SemaphoreType.DMA
    cs = dma((2, NC))
    wall, halo = pl.pallas_call(
        learn_kernel,
        out_shape=(
            jax.ShapeDtypeStruct((2, 2, 2, NC, CH, HALF), bf16),
            jax.ShapeDtypeStruct((ROWS, 2 * HD), bf16),
        ),
        in_specs=[vm] * 4,
        out_specs=(vm, vm),
        scratch_shapes=[
            pltpu.VMEM((4, ROWS, HD), bf16),
            pltpu.VMEM((4 * ROWS, HD), bf16),
            pltpu.VMEM((4 * ROWS, HD), bf16),
            pltpu.VMEM((4 * ROWS, 3 * HALF), bf16),
            pltpu.VMEM((HD, 2 * HALF), f32),
            pltpu.VMEM((HALF, HD), f32),
            pltpu.VMEM((2, NC, CH, HALF), bf16),
            pltpu.VMEM((2, NC, CH, HALF), bf16),
            pltpu.VMEM((2, NC, CH, HALF), f32),
            pltpu.VMEM((2, NC, CH, HALF), bf16),
            pltpu.VMEM((2, NC, 64, 128), f32),
            pltpu.VMEM((2, NC, 64, 128), f32),
            pltpu.VMEM((4 * ROWS, 128), f32),
            pltpu.VMEM((NH, 8, ROWS), f32),
            pltpu.VMEM((NH, 8, ROWS), f32),
            pltpu.VMEM((4, 8, ROWS), f32),
            dma, dma, dma((4,)), dma((4,)), dma((4,)), dma((4,)),
            dma((NH - 1,)), dma((NH,)), dma((3,)), dma((4,)),
            cs, cs, cs, cs, cs, cs, cs, cs,
            cs, cs, cs, cs, cs, cs, dma, dma,
        ],
        compiler_params=pltpu.CompilerParams(collective_id=0, has_side_effects=True),
        name="learn",
    )(tokens, qkv_maps, rate_map, fast_init)
    return pl.pallas_call(
        apply_kernel,
        out_shape=jax.ShapeDtypeStruct((ROWS, 2 * HD), bf16),
        in_specs=[vm] * 4,
        out_specs=vm,
        scratch_shapes=[
            pltpu.VMEM((2 * ROWS, HD), bf16),
            pltpu.VMEM((2 * ROWS, HD), bf16),
        ],
        name="apply",
    )(tokens, halo, qkv_maps, wall)


def solution(mesh):
    in_specs = (
        P("tok", "head"),
        P("head", None, None),
        P("head", None),
        P("head", None, None, None),
    )
    return jax.shard_map(
        body, mesh=mesh, in_specs=in_specs, out_specs=P("tok", "head"), check_vma=False
    )
```

```python
import functools

import jax
import jax.numpy as jnp
from jax import lax
from jax.experimental import pallas as pl
from jax.experimental.pallas import tpu as pltpu
from jax.sharding import PartitionSpec as P

MESH = pl.DeviceIdType.MESH
WINDOW = 512
HD = 512
HALF = 256
ROWS = 512
NC = 8
NT = 16
SUB = 48
SKEW = 4
LAG = 2
NZ = 8
NH = 8
CH = 96

rate_base = 0.003
epsilon = 1e-06

bf16 = jnp.bfloat16
f32 = jnp.float32


def dot(a, b):
    return jnp.dot(a, b, preferred_element_type=f32)


def dot_t(a, b):
    return lax.dot_general(a, b, (((1,), (1,)), ((), ())), preferred_element_type=f32)


def dot_l(a, b):
    return lax.dot_general(a, b, (((0,), (0,)), ((), ())), preferred_element_type=f32)


def softplus(a):
    return jnp.maximum(a, 0.0) + jnp.log1p(jnp.exp(-jnp.abs(a)))


def rms(m):
    m = m.astype(f32)
    return (m * lax.rsqrt(jnp.mean(m * m, axis=-1, keepdims=True) + epsilon)).astype(bf16)


def layer_kernel(
    tok_hbm, maps_hbm, rmap_hbm, init_hbm,
    out_ref,
    tokv, maps, rmap, init, halo, wall,
    xbuf, knb, vb, dbuf, gch, rbuf, sbuf, wcur, ss_s, ss_r,
    rcol, lgs, lgr, rates, kb, vbb, att, qnb,
    in_s,
    xp_s, xp_r, xx_s, xx_r, xf_s, xf_r, lg_s, lg_r, rt_s, rt_r,
    rs_s, rs_r, sp_s, sp_r, wn_s, wn_r, wc_s, wc_r,
    dp_s, dp_r, dx_s, dx_r, df_s, df_r, ha_s, ha_r,
):
    head = lax.axis_index("head")
    tok = lax.axis_index("tok")
    z = tok // 4
    x = (tok // 2) % 2
    c = tok % 2
    p = z % 4
    s = z // 4
    b_me = x * 2 + c
    b_mate = x * 2 + 1 - c
    b_side = (1 - x) * 2 + c
    b_diag = (1 - x) * 2 + 1 - c

    def at(zz, xx, cc):
        return (head, zz * 4 + xx * 2 + cc)

    up = at((z + 1) % NZ, x, c)
    down = at((z + NZ - 1) % NZ, x, c)
    mate = at(z, x, 1 - c)
    side = at(z, 1 - x, c)
    diag = at(z, 1 - x, 1 - c)
    tok_next = (head, (tok + 1) % 32)
    tok_prev = (head, (tok + 31) % 32)

    loads = [
        pltpu.make_async_copy(tok_hbm, tokv, in_s.at[0]),
        pltpu.make_async_copy(rmap_hbm, rmap, in_s.at[1]),
        pltpu.make_async_copy(maps_hbm.at[x], maps.at[x], in_s.at[2]),
        pltpu.make_async_copy(init_hbm.at[x], init, in_s.at[3]),
        pltpu.make_async_copy(maps_hbm.at[1 - x], maps.at[1 - x], in_s.at[4]),
    ]
    for load in loads:
        load.start()

    barrier = pltpu.get_barrier_semaphore()
    peers = [up, down, mate, side, diag, tok_next, tok_prev]
    peers += [((head + o) % NH, tok) for o in range(1, NH)]
    for peer in peers:
        pl.semaphore_signal(barrier, inc=1, device_id=peer, device_id_type=MESH)
    pl.semaphore_wait(barrier, len(peers))

    def rcopy(src, dst, ssem, rsem, dev):
        return pltpu.make_async_remote_copy(
            src_ref=src, dst_ref=dst, send_sem=ssem, recv_sem=rsem,
            device_id=dev, device_id_type=MESH,
        )

    mine = pl.ds(pl.multiple_of(x * HD, HD), HD)
    other = pl.ds(pl.multiple_of((1 - x) * HD, HD), HD)

    def r128(j):
        return pl.ds(pl.multiple_of(j * 128, 128), 128)

    def x_copy(j, b):
        return rcopy(
            tok_hbm.at[r128(j), other], xbuf.at[b, r128(j)], xx_s.at[j], xx_r.at[j], side
        )

    def f_copy(j, b):
        blk = xbuf.at[b, r128(j)]
        return rcopy(blk, blk, xf_s.at[j], xf_r.at[j], mate)

    def p_copy(b):
        return rcopy(tok_hbm.at[:, mine], xbuf.at[b], xp_s, xp_r, mate)

    for j in range(4):
        x_copy(j, b_me).start()
    p_copy(b_me).start()

    loads[0].wait()
    loads[1].wait()
    part = dot_t(rmap[...], tokv[...])
    for q in range(NH):
        lgs[q] = jnp.concatenate([part[2 * q : 2 * q + 2], jnp.zeros((6, ROWS), f32)], 0)

    def lg_copy(o):
        peer = (head + o) % NH
        return rcopy(lgs.at[peer], lgr.at[head], lg_s.at[o - 1], lg_r.at[head], (peer, tok))

    def lg_wait(o):
        src = (head + o) % NH
        return rcopy(lgs.at[src], lgr.at[src], lg_s.at[o - 1], lg_r.at[src], (src, tok))

    for o in range(1, NH):
        lg_copy(o).start()
    lgr[head] = lgs[head]
    xbuf[b_me] = tokv[:, mine]

    cols = pl.ds(pl.multiple_of(c * HALF, HALF), HALF)
    loads[3].wait()

    @pl.when(s == 0)
    def _():
        def fill(j, carry):
            for d in range(2):
                r32 = pl.ds(pl.multiple_of(d * 256 + j * 32, 32), 32)
                r16 = pl.ds(pl.multiple_of(c * HALF + d * 128 + j * 16, 16), 16)
                wcur[d, j, 0:32] = init[0, r32, cols]
                wcur[d, j, 32:64] = init[1, r32, cols]
                wcur[d, j, 64:80] = init[2, r16, 0:HALF]
                wcur[d, j, 80:96] = init[2, r16, HALF:]
            return carry

        lax.fori_loop(0, NC, fill, 0)

    loads[2].wait()

    def keys_values(b, r, n):
        rows = pl.ds(pl.multiple_of(r, n), n)
        xb = xbuf[b, rows]
        out = pl.ds(pl.multiple_of(b * ROWS + r, n), n)
        knb[out] = rms(dot(xb, maps[x, :, HD : 2 * HD]).astype(bf16))
        vb[out] = dot(xb, maps[x, :, 2 * HD :]).astype(bf16)

    def inner(row, n):
        rows = pl.ds(pl.multiple_of(row, n), n)
        kn = knb[rows]
        v = vb[rows]
        w1 = wcur[:, :, 0:32].reshape(HD, HALF)
        w3 = wcur[:, :, 32:64].reshape(HD, HALF)
        w2a = wcur[:, :, 64:80].reshape(HALF, HALF)
        w2b = wcur[:, :, 80:96].reshape(HALF, HALF)
        h1 = dot(kn, w1)
        h3 = dot(kn, w3)
        back = dot_t(v[:, :HALF], w2a) + dot_t(v[:, HALF:], w2b)
        r = rcol[rows]
        r = jnp.concatenate([r, r], 1)
        sig = jax.nn.sigmoid(h1)
        gated = h1 * sig
        back = back * r
        dbuf[rows, 0:HALF] = (back * h3 * sig * (1.0 + h1 * (1.0 - sig))).astype(bf16)
        dbuf[rows, HALF : 2 * HALF] = (back * gated).astype(bf16)
        dbuf[rows, 2 * HALF :] = (gated * h3 * r).astype(bf16)

    def outer(d, row, n, add):
        rows = pl.ds(pl.multiple_of(row, n), n)
        k_cols = pl.ds(pl.multiple_of(d * 256, 256), 256)
        h_cols = pl.ds(pl.multiple_of(2 * HALF + d * 128, 128), 128)
        a = dot_l(knb[rows, k_cols], dbuf[rows, 0 : 2 * HALF])
        e = dot_l(dbuf[rows, h_cols], vb[rows])
        parts = [
            (0, 32, a[:, :HALF]), (32, 32, a[:, HALF:]), (64, 16, e[:, :HALF]), (80, 16, e[:, HALF:])
        ]
        for lo, m, g in parts:
            g = g.reshape(NC, m, HALF)
            if add:
                g = g + gch[d, :, lo : lo + m]
            gch[d, :, lo : lo + m] = g

    def fill_rate(b):
        row = jnp.where(x == 0, rates[b, 0:1], rates[b, 1:2])
        rcol[pl.ds(pl.multiple_of(b * ROWS, ROWS), ROWS)] = jnp.broadcast_to(row, (128, ROWS)).T

    def kv_block(b):
        def step(i, carry):
            keys_values(b, i * 256, 256)
            return carry

        lax.fori_loop(0, 2, step, 0)

    def inner_block(row, n):
        def step(i, carry):
            inner(row + i * 256, 256)
            return carry

        lax.fori_loop(0, n // 256, step, 0)

    kv_block(b_me)
    for o in range(1, NH):
        lg_wait(o).wait_recv()
    total = lgr[0]
    for q in range(1, NH):
        total = total + lgr[q]
    rates[b_me] = (rate_base * softplus(total)).astype(bf16).astype(f32)
    group = [(mate, b_mate), (side, b_side), (diag, b_diag)]

    def rt_copy(i):
        dev, _ = group[i]
        return rcopy(rates.at[b_me], rates.at[b_me], rt_s.at[i], rt_r.at[b_me], dev)

    def rt_wait(i):
        dev, src = group[i]
        return rcopy(rates.at[src], rates.at[src], rt_s.at[i], rt_r.at[src], dev)

    for i in range(3):
        rt_copy(i).start()
    fill_rate(b_me)
    p_copy(b_mate).wait_recv()
    kv_block(b_mate)
    for i in range(3):
        rt_wait(i).wait_recv()
        fill_rate(group[i][1])

    @pl.when(s == 0)
    def _():
        inner_block(x * 2 * ROWS, 2 * ROWS)
        for d in range(2):
            outer(d, x * 2 * ROWS, 2 * ROWS, False)

    def arrive(j, carry):
        @pl.when(j < 4)
        def _():
            x_copy(j, b_side).wait_recv()
            f_copy(j, b_side).start()
            keys_values(b_side, j * 128, 128)

            @pl.when(s == 0)
            def _():
                inner(b_side * ROWS + j * 128, 128)

        @pl.when(j > 0)
        def _():
            f_copy(j - 1, b_diag).wait_recv()
            keys_values(b_diag, (j - 1) * 128, 128)

            @pl.when(s == 0)
            def _():
                inner(b_diag * ROWS + (j - 1) * 128, 128)

        return carry

    lax.fori_loop(0, 5, arrive, 0)

    ha_copy = rcopy(tokv, halo, ha_s, ha_r, tok_next)
    late = (z < 3) & (b_me == 3)

    @pl.when((tok < 31) & jnp.logical_not(late))
    def _():
        ha_copy.start()

    def attention():
        @pl.when(tok == 0)
        def _():
            halo[...] = jnp.zeros_like(halo)

        @pl.when(tok > 0)
        def _():
            ha_copy.wait_recv()

        def one(h, carry):
            lanes = pl.ds(pl.multiple_of(h * HD, HD), HD)

            def kv(i, cc):
                src = pl.ds(pl.multiple_of(i * 256, 256), 256)
                for ref, base in ((halo, 0), (tokv, ROWS)):
                    dst = pl.ds(pl.multiple_of(base + i * 256, 256), 256)
                    xb = ref[src, lanes]
                    kb[dst] = dot(xb, maps[h, :, HD : 2 * HD]).astype(bf16)
                    vbb[dst] = dot(xb, maps[h, :, 2 * HD :]).astype(bf16)
                return cc

            lax.fori_loop(0, 2, kv, 0)

            def block(i, cc):
                rows = pl.ds(pl.multiple_of(i * 256, 256), 256)
                keys = pl.ds(pl.multiple_of(i * 256, 256), 768)
                q = dot(tokv[rows, lanes], maps[h, :, 0:HD]).astype(bf16)
                qnb[rows, lanes] = rms(q)
                sc = dot_t(q, kb[keys]) * (HD ** (-0.5))
                ri = lax.broadcasted_iota(jnp.int32, (256, 768), 0)
                ki = lax.broadcasted_iota(jnp.int32, (256, 768), 1)
                low = jnp.where(tok == 0, WINDOW - i * 256, 0)
                mask = (ki > ri) & (ki <= ri + WINDOW) & (ki >= low)
                top = jnp.max(jnp.where(mask, sc, -1e30), axis=1, keepdims=True)
                e = jnp.where(mask, jnp.exp(sc - top), 0.0)
                probs = (e / jnp.sum(e, axis=1, keepdims=True)).astype(bf16)
                att[rows, lanes] = dot(probs, vbb[keys])
                return cc

            lax.fori_loop(0, 2, block, 0)
            return carry

        lax.fori_loop(0, 2, one, 0)

    def sub(t):
        return t // 2, pl.ds(pl.multiple_of((t % 2) * SUB, 16), SUB)

    def wc_copy(d, t, src):
        j, r = sub(t)
        dev = up if d == 0 else down
        return rcopy(src.at[d, j, r], wcur.at[d, j, r], wc_s.at[d, t], wc_r.at[d, t], dev)

    @pl.when(s == 1)
    def _():
        loads[4].wait()
        attention()

        def step(i, carry):
            for d in range(2):
                hop = z - 4 if d == 0 else 7 - z
                t = i - SKEW * hop

                @pl.when((t >= 0) & (t < NT))
                def _():
                    wc_copy(d, t, wcur).wait_recv()

                    @pl.when(hop < 3)
                    def _():
                        wc_copy(d, t, wcur).start()

            return carry

        lax.fori_loop(0, NT + 3 * SKEW, step, 0)
        inner_block(0, 4 * ROWS)

    def rs_copy(d, t):
        j, r = sub(t)
        dev = up if d == 0 else down
        return rcopy(sbuf.at[d, j, r], rbuf.at[d, j, r], rs_s.at[d, t], rs_r.at[d, t], dev)

    def pos(d):
        return p if d == 0 else 3 - p

    def send_first(d):
        @pl.when(pos(d) == 0)
        def _():
            def step(t, carry):
                j, r = sub(t)
                sbuf[d, j, r] = gch[d, j, r].astype(bf16)
                rs_copy(d, t).start()
                return carry

            lax.fori_loop(0, NT, step, 0)

    def grads(d):
        @pl.when(s == 0)
        def _():
            outer(d, (1 - x) * 2 * ROWS, 2 * ROWS, True)

        @pl.when(s == 1)
        def _():
            outer(d, 0, 4 * ROWS, False)

        send_first(d)

    @pl.when(p < 2)
    def _():
        grads(0)
        grads(1)

    @pl.when(p >= 2)
    def _():
        grads(1)
        grads(0)

    def sp_copy(d, t):
        return rcopy(ss_s.at[d, t], ss_r.at[d, t], sp_s.at[d, t], sp_r.at[d, t], mate)

    def wn_copy(d, t):
        j, r = sub(t)
        dev = down if d == 0 else up
        w = wall.at[x, c, d, j, r]
        return rcopy(w, w, wn_s.at[d, t], wn_r.at[d, t], dev)

    def spread_copy(d, t, xx, cc, ssem, rsem, dev):
        j, r = sub(t)
        w = wall.at[xx, cc, d, j, r]
        return rcopy(w, w, ssem.at[d, t], rsem.at[d, t], dev)

    def dp_copy(d, t, cc):
        return spread_copy(d, t, x, cc, dp_s, dp_r, mate)

    def dx_copy(d, t, xx):
        return spread_copy(d, t, xx, c, dx_s, dx_r, side)

    def df_copy(d, t, cc):
        return spread_copy(d, t, 1 - x, cc, df_s, df_r, mate)

    def spread(d, t):
        dx_copy(d, t, x).start()
        dp_copy(d, t, c).start()

    def rs_stage(d, t):
        q = pos(d)

        @pl.when((t >= 0) & (t < NT) & (q > 0))
        def _():
            j, r = sub(t)
            rs_copy(d, t).wait_recv()
            tot = gch[d, j, r] + rbuf[d, j, r].astype(f32)

            @pl.when(q < 3)
            def _():
                sbuf[d, j, r] = tot.astype(bf16)
                rs_copy(d, t).start()

            @pl.when(q == 3)
            def _():
                w = tot + wcur[d, j, r].astype(f32)
                gch[d, j, r] = w
                sq = w * w
                ss_s[d, t] = sq[:, :128] + sq[:, 128:]
                sp_copy(d, t).start()

    def scale_of(init_rows, have):
        m = init_rows.astype(f32)
        want = jnp.sqrt(jnp.mean(m * m, axis=1, keepdims=True) + epsilon)
        return want / jnp.sqrt(have * (1.0 / HD) + epsilon)

    def fin_stage(d, t):
        @pl.when((t >= 0) & (t < NT) & (pos(d) == 3))
        def _():
            sp_copy(d, t).wait_recv()
            j = t // 2
            have = jnp.sum(ss_s[d, t] + ss_r[d, t], axis=1, keepdims=True)
            r32 = pl.ds(pl.multiple_of(d * 256 + j * 32, 32), 32)
            r16a = pl.ds(pl.multiple_of(d * 256 + j * 32, 16), 16)
            r16b = pl.ds(pl.multiple_of(d * 256 + j * 32 + 16, 16), 16)
            r16 = pl.ds(pl.multiple_of(c * HALF + d * 128 + j * 16, 16), 16)

            @pl.when(t % 2 == 0)
            def _():
                w = gch[d, j, 0:48]
                rows = jnp.concatenate([init[0, r32], init[1, r16a]], 0)
                wall[x, c, d, j, 0:48] = (w * scale_of(rows, have)).astype(bf16)

            @pl.when(t % 2 == 1)
            def _():
                w = gch[d, j, 48:64]
                wall[x, c, d, j, 48:64] = (w * scale_of(init[1, r16b], have[0:16])).astype(bf16)
                wa = gch[d, j, 64:80]
                wb = gch[d, j, 80:96]
                sc = scale_of(init[2, r16], jnp.sum(wa * wa + wb * wb, axis=1, keepdims=True))
                wall[x, c, d, j, 64:80] = (wa * sc).astype(bf16)
                wall[x, c, d, j, 80:96] = (wb * sc).astype(bf16)

            @pl.when(s == 0)
            def _():
                wc_copy(d, t, wall.at[x, c]).start()

            wn_copy(d, t).start()
            spread(d, t)

    def ag_stage(d, t):
        @pl.when((t >= 0) & (t < NT) & (pos(d) < 3))
        def _():
            wn_copy(d, t).wait_recv()

            @pl.when(pos(d) > 0)
            def _():
                wn_copy(d, t).start()

            spread(d, t)

    def pipe(i, carry):
        for d in range(2):
            rs_stage(d, i - SKEW * (pos(d) - 1))
        for d in range(2):
            fin_stage(d, i - 2 * SKEW - LAG)
        for d in range(2):
            ag_stage(d, i - 2 * SKEW - LAG - SKEW * (3 - pos(d)))
        return carry

    lax.fori_loop(0, NT + 5 * SKEW + LAG, pipe, 0)

    @pl.when(late)
    def _():
        ha_copy.start()

    def hand_on(t, carry):
        for d in range(2):
            dx_copy(d, t, 1 - x).wait_recv()
            df_copy(d, t, c).start()
        return carry

    lax.fori_loop(0, NT, hand_on, 0)

    @pl.when(s == 0)
    def _():
        loads[4].wait()
        attention()

    def apply_head(h):
        lanes = pl.ds(pl.multiple_of(h * HD, HD), HD)

        def block(i, cc):
            rows = pl.ds(pl.multiple_of(i * 256, 256), 256)
            qn = qnb[rows, lanes]
            fast = None
            for e in range(2):
                w1 = wall[h, e, :, :, 0:32].reshape(HD, HALF)
                w3 = wall[h, e, :, :, 32:64].reshape(HD, HALF)
                w2a = wall[h, e, :, :, 64:80].reshape(HALF, HALF)
                w2b = wall[h, e, :, :, 80:96].reshape(HALF, HALF)
                a1 = dot(qn, w1)
                hq = (a1 * jax.nn.sigmoid(a1) * dot(qn, w3)).astype(bf16)
                f = jnp.concatenate([dot(hq, w2a), dot(hq, w2b)], 1)
                fast = f if fast is None else fast + f
            out_ref[rows, lanes] = (att[rows, lanes] + fast.astype(bf16).astype(f32)).astype(bf16)
            return cc

        lax.fori_loop(0, 2, block, 0)

    def own_head(t, carry):
        for d in range(2):
            dp_copy(d, t, 1 - c).wait_recv()
        return carry

    lax.fori_loop(0, NT, own_head, 0)
    apply_head(x)

    def other_head(t, carry):
        for d in range(2):
            df_copy(d, t, 1 - c).wait_recv()
        return carry

    lax.fori_loop(0, NT, other_head, 0)
    apply_head(1 - x)

    def finish(t, carry):
        for d in range(2):
            dp_copy(d, t, c).wait_send()
            dx_copy(d, t, x).wait_send()
            df_copy(d, t, c).wait_send()
            q = pos(d)

            @pl.when(q < 3)
            def _():
                rs_copy(d, t).wait_send()

            @pl.when(q == 3)
            def _():
                sp_copy(d, t).wait_send()

            @pl.when(q > 0)
            def _():
                wn_copy(d, t).wait_send()

            hop = z - 4 if d == 0 else 7 - z

            @pl.when(((s == 0) & (q == 3)) | ((s == 1) & (hop < 3)))
            def _():
                wc_copy(d, t, wcur).wait_send()

        return carry

    lax.fori_loop(0, NT, finish, 0)
    p_copy(b_me).wait_send()
    for j in range(4):
        x_copy(j, b_me).wait_send()
        f_copy(j, b_side).wait_send()
    for o in range(1, NH):
        lg_copy(o).wait_send()
    for i in range(3):
        rt_copy(i).wait_send()

    @pl.when(tok < 31)
    def _():
        ha_copy.wait_send()


def body(tokens, qkv_maps, rate_map, fast_init):
    vm = pl.BlockSpec(memory_space=pltpu.VMEM)
    hbm = pl.BlockSpec(memory_space=pl.ANY)
    dma = pltpu.SemaphoreType.DMA
    cs = dma((2, NT))
    V = pltpu.VMEM
    chunk = (2, NC, CH, HALF)
    return pl.pallas_call(
        layer_kernel,
        out_shape=jax.ShapeDtypeStruct((ROWS, 2 * HD), bf16),
        in_specs=[hbm] * 4,
        out_specs=vm,
        scratch_shapes=[
            V((ROWS, 2 * HD), bf16),
            V((2, HD, 3 * HD), bf16),
            V((2 * NH, 2 * HD), bf16),
            V((3, HD, HD), bf16),
            V((ROWS, 2 * HD), bf16),
            V((2, 2) + chunk, bf16),
            V((4, ROWS, HD), bf16),
            V((4 * ROWS, HD), bf16),
            V((4 * ROWS, HD), bf16),
            V((4 * ROWS, 3 * HALF), bf16),
            V(chunk, f32),
            V(chunk, bf16),
            V(chunk, bf16),
            V(chunk, bf16),
            V((2, NT, SUB, 128), f32),
            V((2, NT, SUB, 128), f32),
            V((4 * ROWS, 128), f32),
            V((NH, 8, ROWS), f32),
            V((NH, 8, ROWS), f32),
            V((4, 8, ROWS), f32),
            V((2 * ROWS, HD), bf16),
            V((2 * ROWS, HD), bf16),
            V((ROWS, 2 * HD), f32),
            V((ROWS, 2 * HD), bf16),
            dma((5,)),
            dma, dma, dma((4,)), dma((4,)), dma((4,)), dma((4,)),
            dma((NH - 1,)), dma((NH,)), dma((3,)), dma((4,)),
            cs, cs, cs, cs, cs, cs, cs, cs,
            cs, cs, cs, cs, cs, cs, dma, dma,
        ],
        compiler_params=pltpu.CompilerParams(collective_id=0, has_side_effects=True),
        name="layer",
    )(tokens, qkv_maps, rate_map.T, fast_init)


def solution(mesh):
    in_specs = (
        P("tok", "head"),
        P("head", None, None),
        P("head", None),
        P("head", None, None, None),
    )
    return jax.shard_map(
        body, mesh=mesh, in_specs=in_specs, out_specs=P("tok", "head"), check_vma=False
    )
```
